512 devices in a mesh: rows: 32 (over z_lo, y), blk: 16 (over x, z_hi, core).
Axes of the slice: x: 4, y: 4, z: 16 (z_hi: 2, z_lo: 8; z = z_hi * 8 + z_lo), core: 2. Of those that a mesh axis runs over, the one named last changes fastest.
Arguments:
- features: bfloat16 [131072, 1024], P(('rows', 'blk')), may hold values from -6 to 6
- tiles: bfloat16 [512, 7, 256, 256], P(('rows', 'blk')), may hold values from -0.1875 to 0.1875
- tile_cols: int32 [512, 7], P(('rows', 'blk')), may hold values from 0 to 511, as said below
- tile_count: int32 [512], P(('rows', 'blk')), may hold values from 1 to 7
- weight: bfloat16 [1024, 1024], P(('rows', 'blk')), may hold values from -0.1875 to 0.1875
- cotangent: bfloat16 [131072, 1024], P(('rows', 'blk')), may hold values from -0.0625 to 0.0625
Outputs:
- output: bfloat16 [131072, 1024], P(('rows', 'blk'))
- weight_grad: float32 [1024, 1024], P(('rows', 'blk'))
The draws below stay inside these ranges and needn't reach their ends.
Inputs may be any that keep to these rules, and one draw needn't show every extreme that they name: For each row block g, the first tile_count[g] entries of tile_cols[g] are distinct blocks of g's group of 16 blocks (blocks 16 * (g // 16) onward), each at most 3 positions from g around that group, g itself among them; the later entries are also blocks of that group and carry no tile.
All inputs are finite; a program needn't handle non-finite values.
Results may differ from the reference program's by a relative error of at most 0.0054.
Values may be sent and summed in bfloat16 or wider, within the bound.
A program may use at most 64 MiB of HBM per device.

```python
import jax
import jax.numpy as jnp
from jax import lax

TILE = 256
F = 1024
CYCLE = 16
REACH = 3
TCAP = 7
NBLK = 512
NODES = 131072


def tile_layout(key):
    base = jax.random.fold_in(key, 7)
    key_level, key_rolls = jax.random.split(base, 2)
    level = jax.random.randint(key_level, (NBLK,), 0, 9)
    rolls = jax.random.randint(key_rolls, (NBLK, 2 * REACH), 0, 81)
    bits = (rolls < (level * level)[:, None]).astype(jnp.int32)
    block_ids = jnp.arange(NBLK, dtype=jnp.int32)
    bits = jnp.where(block_ids[:, None] == 0, 1, bits)
    bits = jnp.where(block_ids[:, None] == 1, 0, bits)
    live_all = jnp.concatenate([jnp.ones((NBLK, 1), jnp.int32), bits], axis=1)
    offsets = jnp.concatenate([jnp.zeros((1,), jnp.int32), jnp.arange(-REACH, 0, dtype=jnp.int32), jnp.arange(1, REACH + 1, dtype=jnp.int32)])
    score = (1 - live_all) * TCAP + jnp.arange(TCAP, dtype=jnp.int32)[None, :]
    order = jnp.argsort(score, axis=1, stable=True)
    sorted_off = offsets[order]
    counts = jnp.sum(live_all, axis=1)
    group = block_ids // CYCLE
    local = block_ids % CYCLE
    columns = group[:, None] * CYCLE + (local[:, None] + sorted_off + CYCLE) % CYCLE
    return (columns.astype(jnp.int32), counts.astype(jnp.int32))


def draw_tile_cols(key, part):
    return tile_layout(key)[0]


def draw_tile_count(key, part):
    return tile_layout(key)[1]


def raised(entries, own_key, source, target, parts, factor):
    owner, partner = [(jnp.arange(entries.shape[position]) // (entries.shape[position] // parts)).reshape([-1 if axis == position else 1 for axis in range(entries.ndim)]) for position in (source, target)]
    chosen = jax.random.permutation(own_key, parts)[partner]
    strong = (owner == chosen) | (owner == (partner + parts // 2) % parts)
    return jnp.where(strong, factor * entries, entries)


def level_of(own_key, dims, cuts, low, largest):
    level = 1.0
    for axis_at, shards_of in cuts:
        heights = jax.random.uniform(jax.random.fold_in(jax.random.fold_in(own_key, 6), axis_at), (shards_of,), jnp.float32, low / len(cuts), largest / len(cuts))
        level = level * jnp.repeat(jnp.exp(heights), dims[axis_at] // shards_of).reshape((-1,) + (1,) * (len(dims) - 1 - axis_at))
    return level


def scatter_about(own_key, shape, width, bound, pieces=(), held_as=jnp.bfloat16):
    gain = level_of(own_key, shape, pieces, -0.22, 0.18) if pieces else 1.0
    result = jax.random.normal(own_key, shape, jnp.float32) * width * gain
    return jnp.minimum(jnp.maximum(result, -bound), bound).astype(held_as)


def gaussian_with(own_key, extent, scale, bound, pieces, heavy, kind=jnp.bfloat16):
    drawn = scale * jax.random.normal(own_key, extent, jnp.float32)
    if pieces:
        drawn = drawn * level_of(own_key, extent, pieces, -0.22, 0.18)
    return jnp.clip(raised(drawn, jax.random.fold_in(own_key, 3), *heavy), -bound, bound).astype(kind)


def setup_inputs(seed: int = 0) -> dict:
    streams_of = jax.random.split(jax.random.key(seed), 7)
    features = scatter_about(streams_of[0], (NODES, F), 1.0, 6.0, ((0, 512),))
    tiles = scatter_about(streams_of[1], (NBLK, TCAP, TILE, TILE), (TILE * 4) ** -0.5, 0.1875, ((0, 512),))
    tile_cols = draw_tile_cols(jax.random.fold_in(streams_of[6], 71), 0)
    tile_count = draw_tile_count(jax.random.fold_in(streams_of[6], 71), 0)
    weight = scatter_about(streams_of[4], (F, F), F ** -0.5, 0.1875, ((0, 512),))
    cotangent = gaussian_with(streams_of[5], (NODES, F), NODES ** -0.5, 0.0625, ((0, 512),), (0, 1, 512, 6.0))
    return {"features": features, "tiles": tiles, "tile_cols": tile_cols, "tile_count": tile_count, "weight": weight, "cotangent": cotangent}


def reference(features, tiles, tile_cols, tile_count, weight, cotangent):
    blocks = features.reshape(NBLK, TILE, F)
    slot_ids = jnp.arange(TCAP, dtype=jnp.int32)

    def per_block(block_no):
        columns = tile_cols[block_no]
        gathered = blocks[columns].astype(jnp.float32)
        in_use = (slot_ids < tile_count[block_no]).astype(jnp.float32)
        products = jnp.einsum("kij,kjf->kif", tiles[block_no].astype(jnp.float32), gathered)
        return jnp.einsum("k,kif->if", in_use, products)

    summed = lax.map(per_block, jnp.arange(NBLK, dtype=jnp.int32))
    aggregated = summed.reshape(NODES, F).astype(jnp.bfloat16)
    pre_act = jnp.dot(aggregated, weight.T, preferred_element_type=jnp.float32)
    output = jax.nn.silu(pre_act).astype(jnp.bfloat16)
    sigmoid_y = jax.nn.sigmoid(pre_act)
    grad_pre = (cotangent.astype(jnp.float32) * sigmoid_y * (1.0 + pre_act * (1.0 - sigmoid_y))).astype(jnp.bfloat16)
    weight_grad = jnp.dot(grad_pre.T, aggregated, preferred_element_type=jnp.float32)
    return output, weight_grad
```

```python
import functools

import jax
import jax.numpy as jnp
from jax import lax
from jax.experimental import pallas as pl
from jax.experimental.pallas import tpu as pltpu
from jax.sharding import PartitionSpec as P

MESH = pl.DeviceIdType.MESH
BF = jnp.bfloat16
F32 = jnp.float32
X, Y, Z, C = 4, 4, 16, 2
TILE = 256
F = 1024
SLOTS = 7
CHUNKS = 8
CROWS = TILE // CHUNKS
H = F // 2
PIECE = 2 * Z


def kernel(
    feat, tiles, cols, count, weight, cot, out, wgrad,
    fbuf, tbuf, tsel, cbuf, cperm, onehot, wz, wall, acc, agg, grad, gpart, outp, outv, dw,
    s1x, r1x, s1y, r1y, t2x, t2y, s2x, r2x, s2y, r2y, zs, zr,
    loc, f1s, f1r, f2s, f2r, f3s, f3r, f4s, f4r, f5s, f5r, f6s, f6r,
    wzs, wzr, wys, wyr, wxs, wxr, wps, wpr, ags, agr, gs, gr,
    a1s, a1r, b1s, b1r, a2s, a2r, b2s, b2r, z3s, z3r,
):
    row = lax.axis_index("rows")
    blk = lax.axis_index("blk")
    y = row % Y
    k = blk % C
    zh = (blk // C) % 2
    x = blk // (2 * C)
    z = zh * (Z // 2) + row // Y
    other = 1 - k

    def device(xx, yy, zz, cc):
        return ((zz % (Z // 2)) * Y + yy, (xx * 2 + zz // (Z // 2)) * C + cc)

    partner = device(x, y, z, other)
    far = device(x, y, (z + Z // 2) % Z, k)
    sign = 2 * k - 1
    side = device((x + sign + X) % X, y, z, other)
    step = 1 - 2 * zh
    onward = device((x + step + X) % X, y, z, k)

    def xpeer(d):
        return (x + d) % X

    def ypeer(d):
        return (y + d) % Y

    def zpeer(d):
        return (z + d) % Z

    def remote(src, dst, ss, rs, to):
        return pltpu.make_async_remote_copy(
            src_ref=src, dst_ref=dst, send_sem=ss, recv_sem=rs, device_id=to, device_id_type=MESH
        )

    barrier = pltpu.get_barrier_semaphore()

    def greet(to):
        pl.semaphore_signal(barrier, inc=1, device_id=to, device_id_type=MESH)

    greet(partner)
    greet(side)
    for d in range(1, X):
        greet(device(xpeer(d), y, z, k))
    for d in range(1, Y):
        greet(device(x, ypeer(d), z, k))

    @pl.loop(1, Z)
    def _(d):
        greet(device(x, y, zpeer(d), k))

    own = 4 + k
    load_w = pltpu.make_async_copy(weight, wz.at[z], loc.at[0])
    load_w.start()
    load_f = pltpu.make_async_copy(feat, fbuf.at[own], loc.at[1])
    load_f.start()
    load_t = pltpu.make_async_copy(tiles.at[0], tbuf, loc.at[2])
    load_t.start()
    load_c = pltpu.make_async_copy(cot, cbuf, loc.at[3])
    load_c.start()

    pl.semaphore_wait(barrier, 2 + (X - 1) + (Y - 1) + (Z - 1))

    def wz_copy(d, to):
        return remote(weight, wz.at[to], wzs.at[d], wzr.at[d], device(x, y, zpeer(d), k))

    @pl.loop(1, Z)
    def _(d):
        remote(weight, wz.at[z], wzs.at[d], wzr.at[d], device(x, y, zpeer(d), k)).start()

    same = jnp.where(zh == 1, 0, 2) + k
    cross = jnp.where(zh == 1, 2, 0) + k
    same_there = jnp.where(zh == 1, 2, 0) + k

    def f2(j):
        rows = pl.ds(j * CROWS, CROWS)
        return remote(feat.at[rows], fbuf.at[same_there, rows], f2s.at[j], f2r.at[j], far)

    @pl.loop(0, CHUNKS)
    def _(j):
        f2(j).start()

    f1 = remote(feat, fbuf.at[own], f1s, f1r, partner)
    f1.start()
    f3 = remote(feat, fbuf.at[6], f3s, f3r, side)
    f3.start()

    lane = lax.broadcasted_iota(jnp.int32, (1, F), 1)
    place = (
        (((lane >> 1) & 1) << 9)
        | (((lane >> 5) & 3) << 7)
        | (((lane >> 3) & 3) << 5)
        | (((lane >> 2) & 1) << 4)
        | (((lane >> 7) & 7) << 1)
        | (lane & 1)
    )

    @pl.loop(0, F // 64)
    def _(i):
        rows = lax.broadcasted_iota(jnp.int32, (64, F), 0) + i * 64
        onehot[pl.ds(pl.multiple_of(i * 64, 64), 64), :] = jnp.where(rows == place, 1.0, 0.0).astype(BF)

    load_t.wait()
    live = count[0]
    chip2 = blk - k
    slot_of = []
    for t in range(SLOTS):
        away = (cols[0, t] % (2 * X * C) - chip2 + 2 + 2 * X * C) % (2 * X * C)
        place_t = jnp.where(
            away < 2, away, jnp.where(away < 4, away + 2, jnp.where(away < 6, away - 2, 6))
        )
        slot_of.append(jnp.where(t < live, place_t, -1))
    for s in range(SLOTS):
        which = jnp.int32(0)
        found = jnp.int32(0)
        for t in range(SLOTS):
            hit = slot_of[t] == s
            which = jnp.where(hit, t, which)
            found = jnp.where(hit, 1, found)
        keep = jnp.full((TILE, TILE), found, jnp.int32) == 1
        tsel[:, s * TILE:(s + 1) * TILE] = jnp.where(keep, tbuf[which], jnp.zeros((TILE, TILE), BF))

    load_w.wait()

    @pl.loop(1, Z)
    def _(d):
        remote(weight, wz.at[zpeer(Z - d)], wzs.at[d], wzr.at[d], device(x, y, zpeer(Z - d), k)).wait_recv()

    wall[k, y, x] = wz[...].astype(F32).reshape(PIECE, F).astype(BF)

    def wy(d, dst):
        return remote(
            wall.at[k, dst, x], wall.at[k, dst, x], wys.at[d], wyr.at[d], device(x, ypeer(d), z, k)
        )

    for d in range(1, Y):
        wy(d, y).start()

    load_c.wait()
    for h in range(C):
        cperm[h] = lax.dot_general(
            cbuf[...], onehot[h * H:(h + 1) * H, :], (((1,), (1,)), ((), ())), preferred_element_type=F32
        ).astype(BF)

    for d in range(1, Y):
        wy(d, ypeer(Y - d)).wait_recv()

    def wx(d, dst):
        return remote(
            wall.at[k, :, dst], wall.at[k, :, dst], wxs.at[d], wxr.at[d], device(xpeer(d), y, z, k)
        )

    for d in range(1, X):
        wx(d, x).start()

    load_f.wait()
    remote(feat, fbuf.at[4 + other], f1s, f1r, partner).wait_recv()
    f3.wait_recv()

    @pl.loop(0, F // 256)
    def _(n):
        span = pl.ds(pl.multiple_of(n * 256, 256), 256)
        acc[:, span] = jnp.dot(
            tsel[:, 4 * TILE:], fbuf[4:, :, span].reshape(3 * TILE, 256), preferred_element_type=F32
        )

    def f4(j, slot):
        rows = pl.ds(j * CROWS, CROWS)
        return remote(fbuf.at[slot, rows], fbuf.at[slot, rows], f4s.at[j], f4r.at[j], partner)

    def f5(j, src, dst):
        rows = pl.ds(j * CROWS, CROWS)
        return remote(fbuf.at[src, rows], fbuf.at[dst, rows], f5s.at[j], f5r.at[j], onward)

    def f6(j, slot):
        rows = pl.ds(j * CROWS, CROWS)
        return remote(fbuf.at[slot, rows], fbuf.at[slot, rows], f6s.at[j], f6r.at[j], partner)

    def far_arrival(j):
        rows = pl.ds(j * CROWS, CROWS)
        remote(feat.at[rows], fbuf.at[same, rows], f2s.at[j], f2r.at[j], far).wait_recv()
        f4(j, same).start()
        f5(j, same, cross).start()

    def cross_arrival(j):
        f5(j, same, cross).wait_recv()
        f6(j, cross).start()

    far_arrival(0)

    @pl.loop(1, CHUNKS // 2)
    def _(j):
        far_arrival(j)
        cross_arrival(j - 1)

    for d in range(1, X):
        wx(d, xpeer(X - d)).wait_recv()
    wp = remote(wall.at[k], wall.at[k], wps, wpr, partner)
    wp.start()

    @pl.loop(CHUNKS // 2, CHUNKS)
    def _(j):
        far_arrival(j)
        cross_arrival(j - 1)

    cross_arrival(CHUNKS - 1)
    remote(wall.at[other], wall.at[other], wps, wpr, partner).wait_recv()

    @pl.loop(0, CHUNKS)
    def _(j):
        f4(j, same + other - k).wait_recv()
        f6(j, cross + other - k).wait_recv()

    @pl.loop(0, F // 256)
    def _(n):
        span = pl.ds(pl.multiple_of(n * 256, 256), 256)
        total = acc[:, span] + jnp.dot(
            tsel[:, :4 * TILE], fbuf[:4, :, span].reshape(4 * TILE, 256), preferred_element_type=F32
        )
        agg[0, :, span] = total.astype(BF)

    send_agg = remote(agg.at[0], agg.at[1], ags, agr, partner)
    send_agg.start()

    def half(h):
        for n in range(2):
            pieces = wall[h, 2 * n:2 * n + 2].reshape(256, F)
            pre = lax.dot_general(agg[0], pieces, (((1,), (1,)), ((), ())), preferred_element_type=F32)
            s = jax.nn.sigmoid(pre)
            outp[h, :, n * 256:(n + 1) * 256] = (pre * s).astype(BF)
            ct = cperm[h, :, n * 256:(n + 1) * 256].astype(F32)
            grad[h, :, n * 256:(n + 1) * 256] = (ct * s * (1.0 + pre * (1.0 - s))).astype(BF)

    half(other)
    send_g = remote(grad.at[other], gpart, gs, gr, partner)
    send_g.start()
    half(k)
    send_agg.wait_recv()
    send_g.wait_recv()

    def x1(d, block):
        return remote(s1x.at[block], r1x.at[d], a1s.at[d], a1r.at[d], device(xpeer(d), y, z, k))

    def y1(d, block):
        return remote(s1y.at[block], r1y.at[d], b1s.at[d], b1r.at[d], device(x, ypeer(d), z, k))

    for q in range(Y):
        lanes = slice(q * 128, (q + 1) * 128)
        term = lax.dot_general(
            grad[k, :, lanes], agg[0], (((0,), (0,)), ((), ())), preferred_element_type=F32
        ) + lax.dot_general(gpart[:, lanes], agg[1], (((0,), (0,)), ((), ())), preferred_element_type=F32)
        term = term.reshape(X, PIECE, F)
        dw[q] = term
        for p in range(X):
            s1x[p, q] = term[p, :, :H].astype(BF)
        s1y[q] = term[:, :, H:].astype(BF)

    for d in range(1, X):
        x1(d, xpeer(d)).start()
    for d in range(1, Y):
        y1(d, ypeer(d)).start()

    @pl.loop(0, F // 256)
    def _(n):
        span = pl.ds(pl.multiple_of(n * 256, 256), 256)
        outv[:, span] = (
            jnp.dot(outp[0], onehot[:H, span], preferred_element_type=F32)
            + jnp.dot(outp[1], onehot[H:, span], preferred_element_type=F32)
        ).astype(BF)

    save_out = pltpu.make_async_copy(outv, out, loc.at[4])
    save_out.start()

    for d in range(1, X):
        x1(d, xpeer(d)).wait_recv()
    for q in range(Y):
        total = dw[q, x][:, :H]
        for d in range(1, X):
            total = total + r1x[d, q].astype(F32)
        t2x[q] = total
        s2x[q] = total.astype(BF)

    def y2(d, block):
        return remote(s2x.at[block], r2x.at[d], a2s.at[d], a2r.at[d], device(x, ypeer(d), z, k))

    def x2(d, block):
        return remote(s2y.at[block], r2y.at[d], b2s.at[d], b2r.at[d], device(xpeer(d), y, z, k))

    for d in range(1, Y):
        y2(d, ypeer(d)).start()

    for d in range(1, Y):
        y1(d, ypeer(d)).wait_recv()
    for p in range(X):
        total = dw[y, p][:, H:]
        for d in range(1, Y):
            total = total + r1y[d, p].astype(F32)
        t2y[p] = total
        s2y[p] = total.astype(BF)
    for d in range(1, X):
        x2(d, xpeer(d)).start()

    for d in range(1, Y):
        y2(d, ypeer(d)).wait_recv()
    left = t2x[y]
    for d in range(1, Y):
        left = left + r2x[d].astype(F32)
    zs[:, :, :H] = left.reshape(Z, 2, H)
    for d in range(1, X):
        x2(d, xpeer(d)).wait_recv()
    right = t2y[x]
    for d in range(1, X):
        right = right + r2y[d].astype(F32)
    zs[:, :, H:] = right.reshape(Z, 2, H)

    def z3(d):
        return remote(zs.at[zpeer(d)], zr.at[d], z3s.at[d], z3r.at[d], device(x, y, zpeer(d), k))

    @pl.loop(1, Z)
    def _(d):
        z3(d).start()

    total = zs[z]
    for d in range(1, Z):
        z3(d).wait_recv()
        total = total + zr[d]
    wgrad[...] = total

    @pl.loop(1, Z)
    def _(d):
        wz_copy(d, z).wait_send()
        z3(d).wait_send()

    @pl.loop(0, CHUNKS)
    def _(j):
        f2(j).wait_send()
        f4(j, same).wait_send()
        f5(j, same, cross).wait_send()
        f6(j, cross).wait_send()

    f1.wait_send()
    f3.wait_send()
    wp.wait_send()
    send_agg.wait_send()
    send_g.wait_send()
    for d in range(1, X):
        wx(d, x).wait_send()
        x1(d, xpeer(d)).wait_send()
        x2(d, xpeer(d)).wait_send()
    for d in range(1, Y):
        wy(d, y).wait_send()
        y1(d, ypeer(d)).wait_send()
        y2(d, ypeer(d)).wait_send()
    save_out.wait()


def local(features, tiles, tile_cols, tile_count, weight, cotangent):
    anywhere = pl.BlockSpec(memory_space=pl.ANY)
    scalars = pl.BlockSpec(memory_space=pltpu.SMEM)
    dma = pltpu.SemaphoreType.DMA
    vmem = pltpu.VMEM
    return tuple(pl.pallas_call(
        kernel,
        out_shape=(
            jax.ShapeDtypeStruct((TILE, F), BF),
            jax.ShapeDtypeStruct((2, F), F32),
        ),
        in_specs=[anywhere, anywhere, scalars, scalars, anywhere, anywhere],
        out_specs=(anywhere, pl.BlockSpec(memory_space=pltpu.VMEM)),
        scratch_shapes=[
            vmem((SLOTS, TILE, F), BF),
            vmem((SLOTS, TILE, TILE), BF),
            vmem((TILE, SLOTS * TILE), BF),
            vmem((TILE, F), BF),
            vmem((C, TILE, H), BF),
            vmem((F, F), BF),
            vmem((Z, 2, F), BF),
            vmem((C, Y, X, PIECE, F), BF),
            vmem((TILE, F), F32),
            vmem((C, TILE, F), BF),
            vmem((C, TILE, H), BF),
            vmem((TILE, H), BF),
            vmem((C, TILE, H), BF),
            vmem((TILE, F), BF),
            vmem((Y, X, PIECE, F), F32),
            vmem((X, Y, PIECE, H), BF),
            vmem((X, Y, PIECE, H), BF),
            vmem((Y, X, PIECE, H), BF),
            vmem((Y, X, PIECE, H), BF),
            vmem((Y, PIECE, H), F32),
            vmem((X, PIECE, H), F32),
            vmem((Y, PIECE, H), BF),
            vmem((Y, PIECE, H), BF),
            vmem((X, PIECE, H), BF),
            vmem((X, PIECE, H), BF),
            vmem((Z, 2, F), F32),
            vmem((Z, 2, F), F32),
            dma((5,)),
            dma, dma,
            dma((CHUNKS,)), dma((CHUNKS,)),
            dma, dma,
            dma((CHUNKS,)), dma((CHUNKS,)),
            dma((CHUNKS,)), dma((CHUNKS,)),
            dma((CHUNKS,)), dma((CHUNKS,)),
            dma((Z,)), dma((Z,)),
            dma((Y,)), dma((Y,)),
            dma((X,)), dma((X,)),
            dma, dma,
            dma, dma,
            dma, dma,
            dma((X,)), dma((X,)),
            dma((Y,)), dma((Y,)),
            dma((Y,)), dma((Y,)),
            dma((X,)), dma((X,)),
            dma((Z,)), dma((Z,)),
        ],
        compiler_params=pltpu.CompilerParams(
            collective_id=0, has_side_effects=True, vmem_limit_bytes=56 << 20
        ),
    )(features, tiles, tile_cols, tile_count, weight, cotangent))


def solution(mesh):
    in_specs = (
        P(("rows", "blk"), None),
        P(("rows", "blk"), None, None, None),
        P(("rows", "blk"), None),
        P(("rows", "blk")),
        P(("rows", "blk"), None),
        P(("rows", "blk"), None),
    )
    out_specs = (P(("rows", "blk"), None), P(("rows", "blk"), None))
    return jax.shard_map(local, mesh=mesh, in_specs=in_specs, out_specs=out_specs, check_vma=False)
```

```python
import functools

import jax
import jax.numpy as jnp
from jax import lax
from jax.experimental import pallas as pl
from jax.experimental.pallas import tpu as pltpu
from jax.sharding import PartitionSpec as P

MESH = pl.DeviceIdType.MESH
BF = jnp.bfloat16
F32 = jnp.float32
X, Y, Z, C = 4, 4, 16, 2
TILE = 256
F = 1024
SLOTS = 7
CHUNKS = 8
DEPTH = 2
CROWS = TILE // CHUNKS
H = F // 2
PIECE = 2 * Z


def kernel(
    feat, tiles, cols, count, weight, cot, out, wgrad,
    fbuf, tbuf, tsel, cbuf, cperm, onehot, wz, wall, acc, agg, grad, gpart, outp, outv, dw,
    s1x, r1x, s1y, r1y, t2x, t2y, s2x, r2x, s2y, r2y, zs, zr,
    loc, f1s, f1r, f2s, f2r, f3s, f3r, f4s, f4r, f5s, f5r, f6s, f6r,
    wzs, wzr, wys, wyr, wxs, wxr, wps, wpr, ags, agr, gs, gr,
    a1s, a1r, b1s, b1r, a2s, a2r, b2s, b2r, z3s, z3r,
):
    row = lax.axis_index("rows")
    blk = lax.axis_index("blk")
    y = row % Y
    k = blk % C
    zh = (blk // C) % 2
    x = blk // (2 * C)
    z = zh * (Z // 2) + row // Y
    other = 1 - k

    def device(xx, yy, zz, cc):
        return ((zz % (Z // 2)) * Y + yy, (xx * 2 + zz // (Z // 2)) * C + cc)

    partner = device(x, y, z, other)
    far = device(x, y, (z + Z // 2) % Z, k)
    sign = 2 * k - 1
    side = device((x + sign + X) % X, y, z, other)
    step = 1 - 2 * zh
    onward = device((x + step + X) % X, y, z, k)

    def xpeer(d):
        return (x + d) % X

    def ypeer(d):
        return (y + d) % Y

    def zpeer(d):
        return (z + d) % Z

    def remote(src, dst, ss, rs, to):
        return pltpu.make_async_remote_copy(
            src_ref=src, dst_ref=dst, send_sem=ss, recv_sem=rs, device_id=to, device_id_type=MESH
        )

    barrier = pltpu.get_barrier_semaphore()

    def greet(to):
        pl.semaphore_signal(barrier, inc=1, device_id=to, device_id_type=MESH)

    greet(partner)
    greet(side)
    for d in range(1, X):
        greet(device(xpeer(d), y, z, k))
    for d in range(1, Y):
        greet(device(x, ypeer(d), z, k))

    @pl.loop(1, Z)
    def _(d):
        greet(device(x, y, zpeer(d), k))

    own = 4 + k
    load_w = pltpu.make_async_copy(weight, wz.at[z], loc.at[0])
    load_w.start()
    load_f = pltpu.make_async_copy(feat, fbuf.at[own], loc.at[1])
    load_f.start()
    load_t = pltpu.make_async_copy(tiles.at[0], tbuf, loc.at[2])
    load_t.start()
    load_c = pltpu.make_async_copy(cot, cbuf, loc.at[3])
    load_c.start()

    pl.semaphore_wait(barrier, 2 + (X - 1) + (Y - 1) + (Z - 1))

    def wz_copy(d, to):
        return remote(weight, wz.at[to], wzs.at[d], wzr.at[d], device(x, y, zpeer(d), k))

    @pl.loop(1, Z)
    def _(d):
        remote(weight, wz.at[z], wzs.at[d], wzr.at[d], device(x, y, zpeer(d), k)).start()

    same = jnp.where(zh == 1, 0, 2) + k
    cross = jnp.where(zh == 1, 2, 0) + k
    same_there = jnp.where(zh == 1, 2, 0) + k

    def f2(j):
        rows = pl.ds(j * CROWS, CROWS)
        return remote(feat.at[rows], fbuf.at[same_there, rows], f2s.at[j], f2r.at[j], far)

    @pl.loop(0, DEPTH)
    def _(j):
        f2(j).start()

    f1 = remote(feat, fbuf.at[own], f1s, f1r, partner)
    f1.start()
    f3 = remote(feat, fbuf.at[6], f3s, f3r, side)
    f3.start()

    lane = lax.broadcasted_iota(jnp.int32, (1, F), 1)
    place = (
        (((lane >> 1) & 1) << 9)
        | (((lane >> 5) & 3) << 7)
        | (((lane >> 3) & 3) << 5)
        | (((lane >> 2) & 1) << 4)
        | (((lane >> 7) & 7) << 1)
        | (lane & 1)
    )

    @pl.loop(0, F // 64)
    def _(i):
        rows = lax.broadcasted_iota(jnp.int32, (64, F), 0) + i * 64
        onehot[pl.ds(pl.multiple_of(i * 64, 64), 64), :] = jnp.where(rows == place, 1.0, 0.0).astype(BF)

    load_t.wait()
    live = count[0]
    chip2 = blk - k
    slot_of = []
    for t in range(SLOTS):
        away = (cols[0, t] % (2 * X * C) - chip2 + 2 + 2 * X * C) % (2 * X * C)
        place_t = jnp.where(
            away < 2, away, jnp.where(away < 4, away + 2, jnp.where(away < 6, away - 2, 6))
        )
        slot_of.append(jnp.where(t < live, place_t, -1))
    for s in range(SLOTS):
        which = jnp.int32(0)
        found = jnp.int32(0)
        for t in range(SLOTS):
            hit = slot_of[t] == s
            which = jnp.where(hit, t, which)
            found = jnp.where(hit, 1, found)
        keep = jnp.full((TILE, TILE), found, jnp.int32) == 1
        tsel[:, s * TILE:(s + 1) * TILE] = jnp.where(keep, tbuf[which], jnp.zeros((TILE, TILE), BF))

    load_w.wait()

    @pl.loop(1, Z)
    def _(d):
        remote(weight, wz.at[zpeer(Z - d)], wzs.at[d], wzr.at[d], device(x, y, zpeer(Z - d), k)).wait_recv()

    wall[k, y, x] = wz[...].astype(F32).reshape(PIECE, F).astype(BF)

    def wx(d, dst):
        return remote(
            wall.at[k, y, dst], wall.at[k, y, dst], wxs.at[d], wxr.at[d], device(xpeer(d), y, z, k)
        )

    for d in range(1, X):
        wx(d, x).start()

    load_c.wait()
    for h in range(C):
        cperm[h] = lax.dot_general(
            cbuf[...], onehot[h * H:(h + 1) * H, :], (((1,), (1,)), ((), ())), preferred_element_type=F32
        ).astype(BF)

    for d in range(1, X):
        wx(d, xpeer(X - d)).wait_recv()

    def wy(d, dst):
        return remote(
            wall.at[k, dst], wall.at[k, dst], wys.at[d], wyr.at[d], device(x, ypeer(d), z, k)
        )

    for d in range(1, Y):
        wy(d, y).start()

    load_f.wait()
    remote(feat, fbuf.at[4 + other], f1s, f1r, partner).wait_recv()
    f3.wait_recv()

    @pl.loop(0, F // 256)
    def _(n):
        span = pl.ds(pl.multiple_of(n * 256, 256), 256)
        acc[:, span] = jnp.dot(
            tsel[:, 4 * TILE:], fbuf[4:, :, span].reshape(3 * TILE, 256), preferred_element_type=F32
        )

    def f4(j, slot):
        rows = pl.ds(j * CROWS, CROWS)
        return remote(fbuf.at[slot, rows], fbuf.at[slot, rows], f4s.at[j], f4r.at[j], partner)

    def f5(j, src, dst):
        rows = pl.ds(j * CROWS, CROWS)
        return remote(fbuf.at[src, rows], fbuf.at[dst, rows], f5s.at[j], f5r.at[j], onward)

    def f6(j, slot):
        rows = pl.ds(j * CROWS, CROWS)
        return remote(fbuf.at[slot, rows], fbuf.at[slot, rows], f6s.at[j], f6r.at[j], partner)

    def far_arrival(j):
        rows = pl.ds(j * CROWS, CROWS)
        remote(feat.at[rows], fbuf.at[same, rows], f2s.at[j], f2r.at[j], far).wait_recv()
        f4(j, same).start()
        f5(j, same, cross).start()

        @pl.when(j + DEPTH < CHUNKS)
        def _():
            f2(j).wait_send()
            f2(j + DEPTH).start()

    def cross_arrival(j):
        f5(j, same, cross).wait_recv()
        f6(j, cross).start()

    far_arrival(0)

    @pl.loop(1, CHUNKS // 2)
    def _(j):
        far_arrival(j)
        cross_arrival(j - 1)

    for d in range(1, Y):
        wy(d, ypeer(Y - d)).wait_recv()
    wp = remote(wall.at[k], wall.at[k], wps, wpr, partner)
    wp.start()

    @pl.loop(CHUNKS // 2, CHUNKS)
    def _(j):
        far_arrival(j)
        cross_arrival(j - 1)

    cross_arrival(CHUNKS - 1)
    remote(wall.at[other], wall.at[other], wps, wpr, partner).wait_recv()

    @pl.loop(0, CHUNKS)
    def _(j):
        f4(j, same + other - k).wait_recv()
        f6(j, cross + other - k).wait_recv()

    @pl.loop(0, F // 256)
    def _(n):
        span = pl.ds(pl.multiple_of(n * 256, 256), 256)
        total = acc[:, span] + jnp.dot(
            tsel[:, :4 * TILE], fbuf[:4, :, span].reshape(4 * TILE, 256), preferred_element_type=F32
        )
        agg[0, :, span] = total.astype(BF)

    send_agg = remote(agg.at[0], agg.at[1], ags, agr, partner)
    send_agg.start()

    def half(h):
        for n in range(2):
            pieces = wall[h, 2 * n:2 * n + 2].reshape(256, F)
            pre = lax.dot_general(agg[0], pieces, (((1,), (1,)), ((), ())), preferred_element_type=F32)
            s = jax.nn.sigmoid(pre)
            outp[h, :, n * 256:(n + 1) * 256] = (pre * s).astype(BF)
            ct = cperm[h, :, n * 256:(n + 1) * 256].astype(F32)
            grad[h, :, n * 256:(n + 1) * 256] = (ct * s * (1.0 + pre * (1.0 - s))).astype(BF)

    half(other)
    send_g = remote(grad.at[other], gpart, gs, gr, partner)
    send_g.start()
    half(k)
    send_agg.wait_recv()
    send_g.wait_recv()

    def x1(d, block):
        return remote(s1x.at[block], r1x.at[d], a1s.at[d], a1r.at[d], device(xpeer(d), y, z, k))

    def y1(d, block):
        return remote(s1y.at[block], r1y.at[d], b1s.at[d], b1r.at[d], device(x, ypeer(d), z, k))

    for q in range(Y):
        lanes = slice(q * 128, (q + 1) * 128)
        term = lax.dot_general(
            grad[k, :, lanes], agg[0], (((0,), (0,)), ((), ())), preferred_element_type=F32
        ) + lax.dot_general(gpart[:, lanes], agg[1], (((0,), (0,)), ((), ())), preferred_element_type=F32)
        term = term.reshape(X, PIECE, F)
        dw[q] = term
        for p in range(X):
            s1x[p, q] = term[p, :, :H].astype(BF)
        s1y[q] = term[:, :, H:].astype(BF)

    for d in range(1, X):
        x1(d, xpeer(d)).start()
    for d in range(1, Y):
        y1(d, ypeer(d)).start()

    @pl.loop(0, F // 256)
    def _(n):
        span = pl.ds(pl.multiple_of(n * 256, 256), 256)
        outv[:, span] = (
            jnp.dot(outp[0], onehot[:H, span], preferred_element_type=F32)
            + jnp.dot(outp[1], onehot[H:, span], preferred_element_type=F32)
        ).astype(BF)

    save_out = pltpu.make_async_copy(outv, out, loc.at[4])
    save_out.start()

    for d in range(1, X):
        x1(d, xpeer(d)).wait_recv()
    for q in range(Y):
        total = dw[q, x][:, :H]
        for d in range(1, X):
            total = total + r1x[d, q].astype(F32)
        t2x[q] = total
        s2x[q] = total.astype(BF)

    def y2(d, block):
        return remote(s2x.at[block], r2x.at[d], a2s.at[d], a2r.at[d], device(x, ypeer(d), z, k))

    def x2(d, block):
        return remote(s2y.at[block], r2y.at[d], b2s.at[d], b2r.at[d], device(xpeer(d), y, z, k))

    for d in range(1, Y):
        y2(d, ypeer(d)).start()

    for d in range(1, Y):
        y1(d, ypeer(d)).wait_recv()
    for p in range(X):
        total = dw[y, p][:, H:]
        for d in range(1, Y):
            total = total + r1y[d, p].astype(F32)
        t2y[p] = total
        s2y[p] = total.astype(BF)
    for d in range(1, X):
        x2(d, xpeer(d)).start()

    for d in range(1, Y):
        y2(d, ypeer(d)).wait_recv()
    left = t2x[y]
    for d in range(1, Y):
        left = left + r2x[d].astype(F32)
    zs[:, :, :H] = left.reshape(Z, 2, H)
    for d in range(1, X):
        x2(d, xpeer(d)).wait_recv()
    right = t2y[x]
    for d in range(1, X):
        right = right + r2y[d].astype(F32)
    zs[:, :, H:] = right.reshape(Z, 2, H)

    def z3(d):
        return remote(zs.at[zpeer(d)], zr.at[d], z3s.at[d], z3r.at[d], device(x, y, zpeer(d), k))

    @pl.loop(1, Z)
    def _(d):
        z3(d).start()

    total = zs[z]
    for d in range(1, Z):
        z3(d).wait_recv()
        total = total + zr[d]
    wgrad[...] = total

    @pl.loop(1, Z)
    def _(d):
        wz_copy(d, z).wait_send()
        z3(d).wait_send()

    @pl.loop(0, CHUNKS)
    def _(j):
        f4(j, same).wait_send()
        f5(j, same, cross).wait_send()
        f6(j, cross).wait_send()

    for j in range(CHUNKS - DEPTH, CHUNKS):
        f2(j).wait_send()
    f1.wait_send()
    f3.wait_send()
    wp.wait_send()
    send_agg.wait_send()
    send_g.wait_send()
    for d in range(1, X):
        wx(d, x).wait_send()
        x1(d, xpeer(d)).wait_send()
        x2(d, xpeer(d)).wait_send()
    for d in range(1, Y):
        wy(d, y).wait_send()
        y1(d, ypeer(d)).wait_send()
        y2(d, ypeer(d)).wait_send()
    save_out.wait()


def local(features, tiles, tile_cols, tile_count, weight, cotangent):
    anywhere = pl.BlockSpec(memory_space=pl.ANY)
    scalars = pl.BlockSpec(memory_space=pltpu.SMEM)
    dma = pltpu.SemaphoreType.DMA
    vmem = pltpu.VMEM
    return tuple(pl.pallas_call(
        kernel,
        out_shape=(
            jax.ShapeDtypeStruct((TILE, F), BF),
            jax.ShapeDtypeStruct((2, F), F32),
        ),
        in_specs=[anywhere, anywhere, scalars, scalars, anywhere, anywhere],
        out_specs=(anywhere, pl.BlockSpec(memory_space=pltpu.VMEM)),
        scratch_shapes=[
            vmem((SLOTS, TILE, F), BF),
            vmem((SLOTS, TILE, TILE), BF),
            vmem((TILE, SLOTS * TILE), BF),
            vmem((TILE, F), BF),
            vmem((C, TILE, H), BF),
            vmem((F, F), BF),
            vmem((Z, 2, F), BF),
            vmem((C, Y, X, PIECE, F), BF),
            vmem((TILE, F), F32),
            vmem((C, TILE, F), BF),
            vmem((C, TILE, H), BF),
            vmem((TILE, H), BF),
            vmem((C, TILE, H), BF),
            vmem((TILE, F), BF),
            vmem((Y, X, PIECE, F), F32),
            vmem((X, Y, PIECE, H), BF),
            vmem((X, Y, PIECE, H), BF),
            vmem((Y, X, PIECE, H), BF),
            vmem((Y, X, PIECE, H), BF),
            vmem((Y, PIECE, H), F32),
            vmem((X, PIECE, H), F32),
            vmem((Y, PIECE, H), BF),
            vmem((Y, PIECE, H), BF),
            vmem((X, PIECE, H), BF),
            vmem((X, PIECE, H), BF),
            vmem((Z, 2, F), F32),
            vmem((Z, 2, F), F32),
            dma((5,)),
            dma, dma,
            dma((CHUNKS,)), dma((CHUNKS,)),
            dma, dma,
            dma((CHUNKS,)), dma((CHUNKS,)),
            dma((CHUNKS,)), dma((CHUNKS,)),
            dma((CHUNKS,)), dma((CHUNKS,)),
            dma((Z,)), dma((Z,)),
            dma((Y,)), dma((Y,)),
            dma((X,)), dma((X,)),
            dma, dma,
            dma, dma,
            dma, dma,
            dma((X,)), dma((X,)),
            dma((Y,)), dma((Y,)),
            dma((Y,)), dma((Y,)),
            dma((X,)), dma((X,)),
            dma((Z,)), dma((Z,)),
        ],
        compiler_params=pltpu.CompilerParams(
            collective_id=0, has_side_effects=True, vmem_limit_bytes=56 << 20
        ),
    )(features, tiles, tile_cols, tile_count, weight, cotangent))


def solution(mesh):
    in_specs = (
        P(("rows", "blk"), None),
        P(("rows", "blk"), None, None, None),
        P(("rows", "blk"), None),
        P(("rows", "blk")),
        P(("rows", "blk"), None),
        P(("rows", "blk"), None),
    )
    out_specs = (P(("rows", "blk"), None), P(("rows", "blk"), None))
    return jax.shard_map(local, mesh=mesh, in_specs=in_specs, out_specs=out_specs, check_vma=False)
```
